32 devices in a mesh: fsdp: 8 (over y, x, core), seq: 4 (over z).
Axes of the slice: x: 2, y: 2, z: 4, core: 2. Of those that a mesh axis runs over, the one named last changes fastest.
Arguments:
- latent_in: float32 [8, 512, 1152], P('fsdp', 'seq'), may hold values from -6 to 6
- time_embed: float32 [8, 6912], P('fsdp'), may hold values from -4 to 4
- text_embed: bfloat16 [8, 120, 1152], P('fsdp'), may hold values from -6 to 6
- grad_out: float32 [8, 512, 1152], P('fsdp', 'seq'), may hold values from -6 to 6
- attn_weight: float32 [6, 1152, 1152], P(None, 'fsdp', 'seq'), may hold values from -0.1875 to 0.1875
- attn_first: float32 [6, 1152, 1152], P(None, 'fsdp', 'seq'), may hold values from -20 to 20
- attn_second: float32 [6, 1152, 1152], P(None, 'fsdp', 'seq'), may hold values from 0.4096 to 8.192
- textkv_weight: float32 [2, 1152, 1152], P(None, 'fsdp', 'seq'), may hold values from -0.1875 to 0.1875
- textkv_first: float32 [2, 1152, 1152], P(None, 'fsdp', 'seq'), may hold values from -20 to 20
- textkv_second: float32 [2, 1152, 1152], P(None, 'fsdp', 'seq'), may hold values from 0.4096 to 8.192
- mlp_weight: float32 [2, 1152, 4608], P(None, 'fsdp', 'seq'), may hold values from -0.1875 to 0.1875
- mlp_first: float32 [2, 1152, 4608], P(None, 'fsdp', 'seq'), may hold values from -20 to 20
- mlp_second: float32 [2, 1152, 4608], P(None, 'fsdp', 'seq'), may hold values from 0.4096 to 8.192
- table_weight: float32 [6912], P('seq'), may hold values from -0.4375 to 0.4375
- table_first: float32 [6912], P('seq'), may hold values from -20 to 20
- table_second: float32 [6912], P('seq'), may hold values from 0.4096 to 8.192
Outputs:
- block_out: float32 [8, 512, 1152], P('fsdp', 'seq')
- latent_grad: float32 [8, 512, 1152], P('fsdp', 'seq')
- text_grad: float32 [8, 120, 1152], P('fsdp', None, 'seq')
- time_grad: float32 [8, 6912], P('fsdp', 'seq')
- attn_grad: float32 [6, 1152, 1152], P(None, 'fsdp', 'seq')
- textkv_grad: float32 [2, 1152, 1152], P(None, 'fsdp', 'seq')
- mlp_grad: float32 [2, 1152, 4608], P(None, 'fsdp', 'seq')
- table_grad: float32 [6912], P('seq')
- attn_new: float32 [6, 1152, 1152], P(None, 'fsdp', 'seq')
- textkv_new: float32 [2, 1152, 1152], P(None, 'fsdp', 'seq')
- mlp_new: float32 [2, 1152, 4608], P(None, 'fsdp', 'seq')
- table_new: float32 [6912], P('seq')
- attn_first_new: float32 [6, 1152, 1152], P(None, 'fsdp', 'seq')
- textkv_first_new: float32 [2, 1152, 1152], P(None, 'fsdp', 'seq')
- mlp_first_new: float32 [2, 1152, 4608], P(None, 'fsdp', 'seq')
- table_first_new: float32 [6912], P('seq')
- attn_second_new: float32 [6, 1152, 1152], P(None, 'fsdp', 'seq')
- textkv_second_new: float32 [2, 1152, 1152], P(None, 'fsdp', 'seq')
- mlp_second_new: float32 [2, 1152, 4608], P(None, 'fsdp', 'seq')
- table_second_new: float32 [6912], P('seq')
The draws below stay inside these ranges and needn't reach their ends.
All inputs are finite; a program needn't handle non-finite values.
Results may differ from the reference program's by a relative error of at most 0.025.
Values may be sent and summed in bfloat16 or wider, within the bound.
A program may use at most 192 MiB of HBM per device.

```python
import math
import jax
import jax.numpy as jnp
from jax import lax

D = 1152
HEADS = 16
HEAD_DIM = 72
FF = 4608
TEXT = 120
LAT_TOK = 512
LATENTS = 8


def steps_of(stream_key, shape, shards, low, top_value):
    def one(position, parts):
        heights = jax.random.uniform(jax.random.fold_in(jax.random.fold_in(stream_key, 6), position), (parts,), jnp.float32, low / len(shards), top_value / len(shards))
        return jnp.repeat(jnp.exp(heights), shape[position] // parts).reshape((-1,) + (1,) * (len(shape) - position - 1))

    factor_of = one(*shards[0])
    for cut in shards[1:]:
        factor_of = factor_of * one(*cut)
    return factor_of


def gaussian(key, extent, width, reach, cuts=(), kind=jnp.bfloat16):
    level = steps_of(key, extent, cuts, -0.22, 0.18) if cuts else 1.0
    entries = jax.random.normal(key, extent, jnp.float32) * width * level
    return jnp.minimum(jnp.maximum(entries, -reach), reach).astype(kind)


def setup_inputs(seed: int = 0) -> dict:
    arg_keys = jax.random.split(jax.random.key(seed), 17)
    return {
        "latent_in": gaussian(arg_keys[0], (LATENTS, LAT_TOK, D), 1.0, 6.0, ((0, 8), (1, 4)), jnp.float32),
        "time_embed": gaussian(arg_keys[1], (LATENTS, 6 * D), 0.5, 4.0, ((0, 8),), jnp.float32),
        "text_embed": gaussian(arg_keys[2], (LATENTS, TEXT, D), 1.0, 6.0, ((0, 8),)),
        "grad_out": gaussian(arg_keys[3], (LATENTS, LAT_TOK, D), 1.0, 6.0, ((0, 8), (1, 4)), jnp.float32),
        "attn_weight": gaussian(arg_keys[4], (6, D, D), D ** -0.5, 0.1875, ((1, 8), (2, 4)), jnp.float32),
        "attn_first": gaussian(arg_keys[5], (6, D, D), (0.05 * (LATENTS * LAT_TOK) ** 0.5), 20.0, ((1, 8), (2, 4)), jnp.float32),
        "attn_second": jnp.clip(jnp.exp(math.log(8.192) - 2.9957323 * jax.random.uniform(arg_keys[6], (6, D, D), jnp.float32) ** steps_of(arg_keys[6], (6, D, D), ((1, 8), (2, 4)), -0.2, 0.2)), 0.4096, 8.192),
        "textkv_weight": gaussian(arg_keys[7], (2, D, D), D ** -0.5, 0.1875, ((1, 8), (2, 4)), jnp.float32),
        "textkv_first": gaussian(arg_keys[8], (2, D, D), (0.05 * (LATENTS * LAT_TOK) ** 0.5), 20.0, ((1, 8), (2, 4)), jnp.float32),
        "textkv_second": jnp.clip(jnp.exp(math.log(8.192) - 2.9957323 * jax.random.uniform(arg_keys[9], (2, D, D), jnp.float32) ** steps_of(arg_keys[9], (2, D, D), ((1, 8), (2, 4)), -0.2, 0.2)), 0.4096, 8.192),
        "mlp_weight": gaussian(arg_keys[10], (2, D, FF), D ** -0.5, 0.1875, ((1, 8), (2, 4)), jnp.float32),
        "mlp_first": gaussian(arg_keys[11], (2, D, FF), (0.05 * (LATENTS * LAT_TOK) ** 0.5), 20.0, ((1, 8), (2, 4)), jnp.float32),
        "mlp_second": jnp.clip(jnp.exp(math.log(8.192) - 2.9957323 * jax.random.uniform(arg_keys[12], (2, D, FF), jnp.float32) ** steps_of(arg_keys[12], (2, D, FF), ((1, 8), (2, 4)), -0.2, 0.2)), 0.4096, 8.192),
        "table_weight": gaussian(arg_keys[13], (6 * D,), 0.03, 0.4375, ((0, 4),), jnp.float32),
        "table_first": gaussian(arg_keys[14], (6 * D,), (0.05 * (LATENTS * LAT_TOK) ** 0.5), 20.0, ((0, 4),), jnp.float32),
        "table_second": jnp.clip(jnp.exp(math.log(8.192) - 2.9957323 * jax.random.uniform(arg_keys[15], (6 * D,), jnp.float32) ** steps_of(arg_keys[15], (6 * D,), ((0, 4),), -0.2, 0.2)), 0.4096, 8.192),
    }


norm_eps = 1e-06
gelu_coef = 0.7978845608028654
gelu_cube = 0.044715
beta_first = 0.9
beta_second = 0.999
adam_eps = 1e-08
learn_rate = 0.05
weight_decay = 0.01
fix_first = 1.0 - 0.9 ** 10
fix_second = 1.0 - 0.999 ** 10

def layer_norm(rows):
    centre = rows - lax.optimization_barrier(jnp.mean(rows, axis=-1, keepdims=True))
    recip = lax.rsqrt(lax.optimization_barrier(jnp.mean(centre * centre, axis=-1, keepdims=True)) + norm_eps)
    return (centre * recip, recip)

def norm_back(grad_norm, normed, recip):
    return recip * (grad_norm - lax.optimization_barrier(jnp.mean(grad_norm, axis=-1, keepdims=True)) - normed * lax.optimization_barrier(jnp.mean(grad_norm * normed, axis=-1, keepdims=True)))

def gelu_pair(hidden):
    inner = gelu_coef * (hidden + gelu_cube * hidden * hidden * hidden)
    tangent = jnp.tanh(inner)
    value_out = 0.5 * hidden * (1.0 + tangent)
    slope = 0.5 * (1.0 + tangent) + 0.5 * hidden * (1.0 - tangent * tangent) * gelu_coef * (1.0 + 3.0 * gelu_cube * hidden * hidden)
    return (value_out, slope)

def adamw(weight, moment, second, gradient):
    moment_new = beta_first * moment + (1.0 - beta_first) * gradient
    second_new = beta_second * second + (1.0 - beta_second) * gradient * gradient
    update = moment_new / fix_first / (jnp.sqrt(second_new / fix_second) + adam_eps)
    return (weight - learn_rate * (update + weight_decay * weight), moment_new, second_new)

def matmul(left, right):
    return jnp.dot(left, right, preferred_element_type=jnp.float32)

def attend(query_rows, key_rows, value_rows):
    scores = jnp.einsum('qhd,khd->hqk', query_rows.astype(jnp.float32), key_rows.astype(jnp.float32)) * HEAD_DIM ** (-0.5)
    row_max = lax.optimization_barrier(jnp.max(scores, axis=-1, keepdims=True))
    log_total = row_max + jnp.log(lax.optimization_barrier(jnp.sum(jnp.exp(scores - row_max), axis=-1, keepdims=True)))
    soft_b = jnp.exp(scores - log_total).astype(jnp.bfloat16)
    output = jnp.einsum('hqk,khd->qhd', soft_b.astype(jnp.float32), value_rows.astype(jnp.float32)).astype(jnp.bfloat16)
    return (output, log_total)

def attend_back(query_rows, key_rows, value_rows, log_total, grad_rows):
    scores = jnp.einsum('qhd,khd->hqk', query_rows.astype(jnp.float32), key_rows.astype(jnp.float32)) * HEAD_DIM ** (-0.5)
    soft = jnp.exp(scores - log_total)
    grad_soft = jnp.einsum('qhd,khd->hqk', grad_rows.astype(jnp.float32), value_rows.astype(jnp.float32))
    row_dot = lax.optimization_barrier(jnp.sum(soft * grad_soft, axis=-1, keepdims=True))
    grad_score = (soft * (grad_soft - row_dot) * HEAD_DIM ** (-0.5)).astype(jnp.bfloat16).astype(jnp.float32)
    grad_query = jnp.einsum('hqk,khd->qhd', grad_score, key_rows.astype(jnp.float32)).astype(jnp.bfloat16)
    grad_key = jnp.einsum('hqk,qhd->khd', grad_score, query_rows.astype(jnp.float32)).astype(jnp.bfloat16)
    soft_b = soft.astype(jnp.bfloat16).astype(jnp.float32)
    grad_value = jnp.einsum('hqk,qhd->khd', soft_b, grad_rows.astype(jnp.float32)).astype(jnp.bfloat16)
    return (grad_query, grad_key, grad_value)

def one_latent(latent, time_row, text_rows, grad_rows, attn_b, text_b, mlp_b, table_b):
    length = latent.shape[0]
    modulation = (time_row + table_b.astype(jnp.float32)).reshape(6, D)
    shift_one, scale_one, gate_one, shift_two, scale_two, gate_two = jnp.split(modulation, 6, axis=0)
    normed_one, recip_one = layer_norm(latent)
    mod_one = (normed_one * (1.0 + scale_one) + shift_one).astype(jnp.bfloat16)
    query_rows = matmul(mod_one, attn_b[0]).astype(jnp.bfloat16).reshape(length, HEADS, HEAD_DIM)
    key_rows = matmul(mod_one, attn_b[1]).astype(jnp.bfloat16).reshape(length, HEADS, HEAD_DIM)
    value_rows = matmul(mod_one, attn_b[2]).astype(jnp.bfloat16).reshape(length, HEADS, HEAD_DIM)
    self_out, self_total = attend(query_rows, key_rows, value_rows)
    self_flat = self_out.reshape(length, D)
    branch = matmul(self_flat, attn_b[3])
    after_self = latent + gate_one * branch
    after_self_b = after_self.astype(jnp.bfloat16)
    cross_query = matmul(after_self_b, attn_b[4]).astype(jnp.bfloat16).reshape(length, HEADS, HEAD_DIM)
    text_keys = matmul(text_rows, text_b[0]).astype(jnp.bfloat16).reshape(TEXT, HEADS, HEAD_DIM)
    text_values = matmul(text_rows, text_b[1]).astype(jnp.bfloat16).reshape(TEXT, HEADS, HEAD_DIM)
    cross_out, cross_total = attend(cross_query, text_keys, text_values)
    cross_flat = cross_out.reshape(length, D)
    after_cross = after_self + matmul(cross_flat, attn_b[5])
    normed_two, recip_two = layer_norm(after_cross)
    mod_two = (normed_two * (1.0 + scale_two) + shift_two).astype(jnp.bfloat16)
    hidden = matmul(mod_two, mlp_b[0])
    activated, slope = gelu_pair(hidden)
    activated_b = activated.astype(jnp.bfloat16)
    mlp_out = matmul(activated_b, mlp_b[1].T)
    block_out = after_cross + gate_two * mlp_out
    grad_gate_two = lax.optimization_barrier(jnp.sum(grad_rows * mlp_out, axis=0, keepdims=True))
    grad_mlp = (gate_two * grad_rows).astype(jnp.bfloat16)
    grad_down = matmul(grad_mlp.T, activated_b)
    grad_hidden = (matmul(grad_mlp, mlp_b[1]) * slope).astype(jnp.bfloat16)
    grad_up = matmul(mod_two.T, grad_hidden)
    grad_mod_two = matmul(grad_hidden, mlp_b[0].T)
    grad_scale_two = lax.optimization_barrier(jnp.sum(grad_mod_two * normed_two, axis=0, keepdims=True))
    grad_shift_two = lax.optimization_barrier(jnp.sum(grad_mod_two, axis=0, keepdims=True))
    grad_cross = grad_rows + norm_back(grad_mod_two * (1.0 + scale_two), normed_two, recip_two)
    grad_cross_b = grad_cross.astype(jnp.bfloat16)
    grad_cproj = matmul(cross_flat.T, grad_cross_b)
    grad_cross_out = matmul(grad_cross_b, attn_b[5].T).astype(jnp.bfloat16).reshape(length, HEADS, HEAD_DIM)
    grad_cq, grad_tk, grad_tv = attend_back(cross_query, text_keys, text_values, cross_total, grad_cross_out)
    grad_cq_flat = grad_cq.reshape(length, D)
    grad_tk_flat = grad_tk.reshape(TEXT, D)
    grad_tv_flat = grad_tv.reshape(TEXT, D)
    grad_cquery_w = matmul(after_self_b.T, grad_cq_flat)
    grad_self = grad_cross + matmul(grad_cq_flat, attn_b[4].T)
    grad_tkey_w = matmul(text_rows.T, grad_tk_flat)
    grad_tval_w = matmul(text_rows.T, grad_tv_flat)
    grad_text = matmul(grad_tk_flat, text_b[0].T) + matmul(grad_tv_flat, text_b[1].T)
    grad_gate_one = lax.optimization_barrier(jnp.sum(grad_self * branch, axis=0, keepdims=True))
    grad_branch = (gate_one * grad_self).astype(jnp.bfloat16)
    grad_proj = matmul(self_flat.T, grad_branch)
    grad_self_out = matmul(grad_branch, attn_b[3].T).astype(jnp.bfloat16).reshape(length, HEADS, HEAD_DIM)
    grad_q, grad_k, grad_v = attend_back(query_rows, key_rows, value_rows, self_total, grad_self_out)
    grad_q_flat = grad_q.reshape(length, D)
    grad_k_flat = grad_k.reshape(length, D)
    grad_v_flat = grad_v.reshape(length, D)
    grad_wq = matmul(mod_one.T, grad_q_flat)
    grad_wk = matmul(mod_one.T, grad_k_flat)
    grad_wv = matmul(mod_one.T, grad_v_flat)
    grad_mod_one = matmul(grad_q_flat, attn_b[0].T) + matmul(grad_k_flat, attn_b[1].T) + matmul(grad_v_flat, attn_b[2].T)
    grad_scale_one = lax.optimization_barrier(jnp.sum(grad_mod_one * normed_one, axis=0, keepdims=True))
    grad_shift_one = lax.optimization_barrier(jnp.sum(grad_mod_one, axis=0, keepdims=True))
    grad_latent = grad_self + norm_back(grad_mod_one * (1.0 + scale_one), normed_one, recip_one)
    grad_time = jnp.concatenate([grad_shift_one, grad_scale_one, grad_gate_one, grad_shift_two, grad_scale_two, grad_gate_two], axis=0).reshape(6 * D)
    grad_attn = jnp.stack([grad_wq, grad_wk, grad_wv, grad_proj, grad_cquery_w, grad_cproj])
    grad_textkv = jnp.stack([grad_tkey_w, grad_tval_w])
    grad_mlpw = jnp.stack([grad_up, grad_down])
    return (block_out, grad_latent, grad_text, grad_time, grad_attn, grad_textkv, grad_mlpw)

def reference(latent_in, time_embed, text_embed, grad_out, attn_weight, attn_first, attn_second, textkv_weight, textkv_first, textkv_second, mlp_weight, mlp_first, mlp_second, table_weight, table_first, table_second):
    attn_b = attn_weight.astype(jnp.bfloat16)
    text_b = textkv_weight.astype(jnp.bfloat16)
    mlp_b = mlp_weight.astype(jnp.bfloat16)
    table_b = table_weight.astype(jnp.bfloat16)

    def scan_step(carry, item):
        latent, time_row, text_rows, grad_rows = item
        results = one_latent(latent, time_row, text_rows, grad_rows, attn_b, text_b, mlp_b, table_b)
        carry = (carry[0] + results[4], carry[1] + results[5], carry[2] + results[6])
        return (carry, results[:4])
    zeros = (jnp.zeros(attn_weight.shape, jnp.float32), jnp.zeros(textkv_weight.shape, jnp.float32), jnp.zeros(mlp_weight.shape, jnp.float32))
    grads, stacked = lax.scan(scan_step, zeros, (latent_in, time_embed, text_embed, grad_out))
    attn_grad, textkv_grad, mlp_grad = grads
    block_out, latent_grad, text_grad, time_grad = stacked
    table_grad = lax.optimization_barrier(jnp.sum(time_grad, axis=0))
    attn_new, attn_first_new, attn_second_new = adamw(attn_weight, attn_first, attn_second, attn_grad)
    textkv_new, textkv_first_new, textkv_second_new = adamw(textkv_weight, textkv_first, textkv_second, textkv_grad)
    mlp_new, mlp_first_new, mlp_second_new = adamw(mlp_weight, mlp_first, mlp_second, mlp_grad)
    table_new, table_first_new, table_second_new = adamw(table_weight, table_first, table_second, table_grad)
    return (block_out, latent_grad, text_grad, time_grad, attn_grad, textkv_grad, mlp_grad, table_grad, attn_new, textkv_new, mlp_new, table_new, attn_first_new, textkv_first_new, mlp_first_new, table_first_new, attn_second_new, textkv_second_new, mlp_second_new, table_second_new)
```

```python
import functools
import math

import jax
import jax.numpy as jnp
from jax import lax
from jax.experimental import pallas as pl
from jax.experimental.pallas import tpu as pltpu
from jax.sharding import PartitionSpec as P

HEAD_DIM = 72


norm_eps = 1e-06
gelu_coef = 0.7978845608028654
gelu_cube = 0.044715
beta_first = 0.9
beta_second = 0.999
adam_eps = 1e-08
learn_rate = 0.05
weight_decay = 0.01
fix_first = 1.0 - 0.9**10
fix_second = 1.0 - 0.999**10


def layer_norm(rows):
    centre = rows - jnp.mean(rows, axis=-1, keepdims=True)
    recip = lax.rsqrt(jnp.mean(centre * centre, axis=-1, keepdims=True) + norm_eps)
    return (centre * recip, recip)


def norm_back(grad_norm, normed, recip):
    return recip * (
        grad_norm
        - jnp.mean(grad_norm, axis=-1, keepdims=True)
        - normed * jnp.mean(grad_norm * normed, axis=-1, keepdims=True)
    )


def gelu_pair(hidden):
    inner = gelu_coef * (hidden + gelu_cube * hidden * hidden * hidden)
    tangent = jnp.tanh(inner)
    value_out = 0.5 * hidden * (1.0 + tangent)
    slope = 0.5 * (1.0 + tangent) + 0.5 * hidden * (1.0 - tangent * tangent) * gelu_coef * (
        1.0 + 3.0 * gelu_cube * hidden * hidden
    )
    return (value_out, slope)


def adamw(weight, moment, second, gradient):
    moment_new = beta_first * moment + (1.0 - beta_first) * gradient
    second_new = beta_second * second + (1.0 - beta_second) * gradient * gradient
    update = moment_new / fix_first / (jnp.sqrt(second_new / fix_second) + adam_eps)
    return (weight - learn_rate * (update + weight_decay * weight), moment_new, second_new)


def line_gather_kernel(n, count, *refs):
    sources, targets = refs[:count], refs[count : 2 * count]
    local_sem, send_right, recv_right, send_left, recv_left = refs[2 * count :]
    me = lax.axis_index("seq")
    barrier = pltpu.get_barrier_semaphore()

    @pl.when(me > 0)
    def _():
        pl.semaphore_signal(barrier, inc=1, device_id={"seq": me - 1})

    @pl.when(me < n - 1)
    def _():
        pl.semaphore_signal(barrier, inc=1, device_id={"seq": me + 1})

    own = [
        pltpu.make_async_copy(source, target.at[me], local_sem.at[item])
        for item, (source, target) in enumerate(zip(sources, targets))
    ]
    for copy in own:
        copy.start()

    pl.semaphore_wait(barrier, jnp.where(me > 0, 1, 0) + jnp.where(me < n - 1, 1, 0))

    def hop(item, step, right):
        block = me - step if right else me + step
        source = sources[item] if step == 0 else targets[item].at[block]
        sends, receives = (send_right, recv_right) if right else (send_left, recv_left)
        return pltpu.make_async_remote_copy(
            src_ref=source,
            dst_ref=targets[item].at[block],
            send_sem=sends.at[item, step],
            recv_sem=receives.at[item, step],
            device_id={"seq": me + 1 if right else me - 1},
        )

    def arrival(item, step, right):
        block = me - 1 - step if right else me + 1 + step
        sends, receives = (send_right, recv_right) if right else (send_left, recv_left)
        return pltpu.make_async_copy(
            sources[item], targets[item].at[block], receives.at[item, step]
        )

    def sends_right(step):
        return jnp.logical_and(me - step >= 0, me < n - 1)

    def sends_left(step):
        return jnp.logical_and(me + step < n, me > 0)

    for step in range(n - 1):
        for item in range(count):

            @pl.when(sends_right(step))
            def _():
                hop(item, step, True).start()

            @pl.when(sends_left(step))
            def _():
                hop(item, step, False).start()

        for item in range(count):

            @pl.when(me - 1 - step >= 0)
            def _():
                arrival(item, step, True).wait()

            @pl.when(me + 1 + step < n)
            def _():
                arrival(item, step, False).wait()

    for step in range(n - 1):
        for item in range(count):

            @pl.when(sends_right(step))
            def _():
                hop(item, step, True).wait_send()

            @pl.when(sends_left(step))
            def _():
                hop(item, step, False).wait_send()

    for copy in own:
        copy.wait()


def line_gather(ident, *arrays):
    n = lax.axis_size("seq")
    count = len(arrays)
    anywhere = pl.BlockSpec(memory_space=pl.ANY)
    return pl.pallas_call(
        functools.partial(line_gather_kernel, n, count),
        out_shape=[jax.ShapeDtypeStruct((n,) + a.shape, a.dtype) for a in arrays],
        in_specs=[anywhere] * count,
        out_specs=[anywhere] * count,
        scratch_shapes=[pltpu.SemaphoreType.DMA((count,))]
        + [pltpu.SemaphoreType.DMA((count, n - 1))] * 4,
        compiler_params=pltpu.CompilerParams(collective_id=ident, has_side_effects=True),
    )(*arrays)


def attend(query_rows, key_rows, value_rows, block):
    latents, length, group, width = query_rows.shape
    count = length // block
    pieces = jnp.moveaxis(query_rows.reshape(latents, count, block, group, width), 1, 0)

    def one_block(piece):
        scores = jnp.einsum(
            "bqgd,bkgd->bgqk", piece, key_rows, preferred_element_type=jnp.float32
        ) * width ** (-0.5)
        row_max = jnp.max(scores, axis=-1, keepdims=True)
        log_total = row_max + jnp.log(jnp.sum(jnp.exp(scores - row_max), axis=-1, keepdims=True))
        soft_b = jnp.exp(scores - log_total).astype(jnp.bfloat16)
        output = jnp.einsum(
            "bgqk,bkgd->bqgd", soft_b, value_rows, preferred_element_type=jnp.float32
        ).astype(jnp.bfloat16)
        return (output, log_total)

    outputs, totals = lax.map(one_block, pieces)
    return (jnp.moveaxis(outputs, 0, 1).reshape(query_rows.shape), totals)


def attend_back(query_rows, key_rows, value_rows, totals, grad_rows, block):
    latents, length, group, width = query_rows.shape
    count = length // block
    query_pieces = jnp.moveaxis(query_rows.reshape(latents, count, block, group, width), 1, 0)
    grad_pieces = jnp.moveaxis(grad_rows.reshape(latents, count, block, group, width), 1, 0)

    def one_block(carry, item):
        piece, grad_piece, log_total = item
        scores = jnp.einsum(
            "bqgd,bkgd->bgqk", piece, key_rows, preferred_element_type=jnp.float32
        ) * width ** (-0.5)
        soft = jnp.exp(scores - log_total)
        grad_soft = jnp.einsum(
            "bqgd,bkgd->bgqk", grad_piece, value_rows, preferred_element_type=jnp.float32
        )
        row_dot = jnp.sum(soft * grad_soft, axis=-1, keepdims=True)
        grad_score = (soft * (grad_soft - row_dot) * width ** (-0.5)).astype(jnp.bfloat16)
        grad_query = jnp.einsum(
            "bgqk,bkgd->bqgd", grad_score, key_rows, preferred_element_type=jnp.float32
        ).astype(jnp.bfloat16)
        grad_key = carry[0] + jnp.einsum(
            "bgqk,bqgd->bkgd", grad_score, piece, preferred_element_type=jnp.float32
        )
        grad_value = carry[1] + jnp.einsum(
            "bgqk,bqgd->bkgd",
            soft.astype(jnp.bfloat16),
            grad_piece,
            preferred_element_type=jnp.float32,
        )
        return ((grad_key, grad_value), grad_query)

    zeros = jnp.zeros(key_rows.shape, jnp.float32)
    (grad_key, grad_value), grad_query = lax.scan(
        one_block, (zeros, zeros), (query_pieces, grad_pieces, totals)
    )
    grad_query = jnp.moveaxis(grad_query, 0, 1).reshape(query_rows.shape)
    return (grad_query, grad_key.astype(jnp.bfloat16), grad_value.astype(jnp.bfloat16))


def body(
    latent_in,
    time_embed,
    text_embed,
    grad_out,
    attn_weight,
    attn_first,
    attn_second,
    textkv_weight,
    textkv_first,
    textkv_second,
    mlp_weight,
    mlp_first,
    mlp_second,
    table_weight,
    table_first,
    table_second,
):
    n_seq = lax.axis_size("seq")
    me = lax.axis_index("seq")
    latents, tokens, width = latent_in.shape
    text_len = text_embed.shape[1]
    length = tokens * n_seq
    group_width = width // n_seq
    group = group_width // HEAD_DIM
    block = math.gcd(length, 512)
    f32, bf16 = jnp.float32, jnp.bfloat16
    attn_b = attn_weight.astype(bf16)
    text_b = textkv_weight.astype(bf16)

    def dot(spec, left, right):
        return jnp.einsum(spec, left, right, preferred_element_type=f32)

    def join_tokens(blocks):
        return jnp.moveaxis(blocks, 0, 1).reshape(latents, length, blocks.shape[-1])

    def own_tokens(rows):
        return lax.dynamic_slice_in_dim(rows, me * tokens, tokens, axis=1)

    cols_full = lax.all_gather(
        jnp.concatenate([attn_b[0:3], text_b, attn_b[4:5]], axis=0), "fsdp", axis=1, tiled=True
    )
    out_pieces, latent_all, table_all = line_gather(
        0,
        jnp.stack([attn_b[3], attn_b[5]]),
        latent_in.astype(bf16),
        table_weight.astype(bf16)[None, :],
    )
    out_rows = jnp.moveaxis(out_pieces, 0, 2).reshape(2, attn_b.shape[1], width)
    out_rows, cols_full = lax.optimization_barrier((out_rows, cols_full))
    out_full = lax.all_gather(out_rows, "fsdp", axis=1, tiled=True)
    mlp_b, out_full = lax.optimization_barrier((mlp_weight.astype(bf16), out_full))
    mlp_full = lax.all_gather(mlp_b, "fsdp", axis=1, tiled=True)

    modulation = (time_embed + table_all.reshape(1, -1).astype(f32)).reshape(latents, 6, width)
    shift_one, scale_one, gate_one, shift_two, scale_two, gate_two = jnp.split(
        modulation, 6, axis=1
    )
    latent_rows = join_tokens(latent_all).astype(f32)
    normed_rows, _ = layer_norm(latent_rows)
    mod_rows_one = (normed_rows * (1.0 + scale_one) + shift_one).astype(bf16)
    qkv = dot("bld,sde->sble", mod_rows_one, cols_full[0:3]).astype(bf16)
    query_rows = qkv[0].reshape(latents, length, group, HEAD_DIM)
    key_rows = qkv[1].reshape(latents, length, group, HEAD_DIM)
    value_rows = qkv[2].reshape(latents, length, group, HEAD_DIM)
    self_out, self_total = attend(query_rows, key_rows, value_rows, block)
    self_all, grad_all, cquery_pieces = line_gather(
        1,
        self_out.reshape(latents, length, group_width),
        grad_out.astype(bf16),
        attn_b[4],
    )
    proj_rows = out_full[0].reshape(n_seq, group_width, width)
    cproj_rows = out_full[1].reshape(n_seq, group_width, width)
    branch = dot("nblc,nce->ble", self_all, proj_rows)
    after_self = latent_rows + gate_one * branch
    after_self_b = after_self.astype(bf16)
    cross_query = (
        dot("bld,de->ble", after_self_b, cols_full[5])
        .astype(bf16)
        .reshape(latents, length, group, HEAD_DIM)
    )
    text_kv = dot("bsd,mde->mbse", text_embed, cols_full[3:5]).astype(bf16)
    text_keys = text_kv[0].reshape(latents, text_len, group, HEAD_DIM)
    text_values = text_kv[1].reshape(latents, text_len, group, HEAD_DIM)
    cross_out, cross_total = attend(cross_query, text_keys, text_values, block)
    (cross_all,) = line_gather(2, cross_out.reshape(latents, length, group_width))
    cross_branch = dot("nblc,nce->ble", cross_all, cproj_rows)
    after_cross = after_self + cross_branch
    own_branch = own_tokens(branch)
    own_after = latent_in + gate_one * own_branch + own_tokens(cross_branch)
    normed_two, recip_two = layer_norm(own_after)
    normed_all, _ = layer_norm(after_cross)
    mod_rows = (normed_all * (1.0 + scale_two) + shift_two).astype(bf16)
    hidden = dot("bld,df->blf", mod_rows, mlp_full[0])
    activated, slope = gelu_pair(hidden)
    activated_b = activated.astype(bf16)
    grad_mlp_rows = (gate_two * join_tokens(grad_all).astype(f32)).astype(bf16)
    grad_act = dot("bld,df->blf", grad_mlp_rows, mlp_full[1])
    grad_hidden = (grad_act * slope).astype(bf16)
    grad_mod_part = dot("blf,df->bld", grad_hidden, mlp_full[0])
    grad_mod_two = lax.psum_scatter(
        grad_mod_part.astype(bf16), "seq", scatter_dimension=1, tiled=True
    ).astype(f32)
    grad_down = dot("bld,blf->df", grad_mlp_rows, activated_b)
    grad_up = dot("bld,blf->df", mod_rows, grad_hidden)
    partial_out = dot("blf,df->bld", activated_b, mlp_full[1]).astype(bf16)
    grad_mlp_part = jnp.stack([grad_up.astype(bf16), grad_down.astype(bf16)])
    grad_mod_two, partial_out, grad_mlp_part, cquery_pieces = lax.optimization_barrier(
        (grad_mod_two, partial_out, grad_mlp_part, cquery_pieces)
    )
    cquery_full = lax.all_gather(cquery_pieces, "fsdp", axis=1, tiled=True)
    grad_scale_two = jnp.sum(grad_mod_two * normed_two, axis=1, keepdims=True)
    grad_shift_two = jnp.sum(grad_mod_two, axis=1, keepdims=True)
    grad_cross = grad_out + norm_back(grad_mod_two * (1.0 + scale_two), normed_two, recip_two)
    (grad_cross_all,) = line_gather(3, grad_cross.astype(bf16))
    grad_cross_b = join_tokens(grad_cross_all)
    own_cproj = lax.dynamic_index_in_dim(cproj_rows, me, axis=0, keepdims=False)
    own_proj = lax.dynamic_index_in_dim(proj_rows, me, axis=0, keepdims=False)
    grad_cross_heads = (
        dot("ble,ce->blc", grad_cross_b, own_cproj)
        .astype(bf16)
        .reshape(latents, length, group, HEAD_DIM)
    )
    grad_cq, grad_tk, grad_tv = attend_back(
        cross_query, text_keys, text_values, cross_total, grad_cross_heads, block
    )
    grad_cq = grad_cq.reshape(latents, length, group_width)
    grad_cq_blocks = lax.all_to_all(
        jnp.moveaxis(grad_cq.reshape(latents, n_seq, tokens, group_width), 1, 0),
        "seq",
        split_axis=0,
        concat_axis=0,
        tiled=True,
    )
    cquery_full, grad_mlp_part, partial_out = lax.optimization_barrier(
        (cquery_full, grad_mlp_part, partial_out)
    )
    mlp_grad = lax.psum_scatter(
        grad_mlp_part, "fsdp", scatter_dimension=1, tiled=True
    ).astype(f32)
    mlp_out = lax.psum_scatter(partial_out, "seq", scatter_dimension=1, tiled=True).astype(f32)
    grad_self = grad_cross + dot("nbtc,ndc->btd", grad_cq_blocks, cquery_full)
    block_out = own_after + gate_two * mlp_out
    grad_gate_two = jnp.sum(grad_out * mlp_out, axis=1, keepdims=True)
    grad_gate_one = jnp.sum(grad_self * own_branch, axis=1, keepdims=True)
    (grad_branch_all,) = line_gather(4, (gate_one * grad_self).astype(bf16))
    grad_branch = join_tokens(grad_branch_all)
    grad_self_heads = (
        dot("ble,ce->blc", grad_branch, own_proj)
        .astype(bf16)
        .reshape(latents, length, group, HEAD_DIM)
    )
    grad_q, grad_k, grad_v = attend_back(
        query_rows, key_rows, value_rows, self_total, grad_self_heads, block
    )
    grad_qkv = jnp.stack([item.reshape(latents, length, group_width) for item in (grad_q, grad_k, grad_v)])
    grad_mod_one_part = dot("sble,sde->bld", grad_qkv, cols_full[0:3])
    grad_tk = grad_tk.reshape(latents, text_len, group_width)
    grad_tv = grad_tv.reshape(latents, text_len, group_width)
    grad_text_kv = jnp.stack([grad_tk, grad_tv])
    grad_text_part = dot("mbse,mde->bsd", grad_text_kv, cols_full[3:5])
    grad_scale_one = jnp.sum(grad_mod_one_part * normed_rows, axis=1, keepdims=True)
    grad_shift_one = jnp.sum(grad_mod_one_part, axis=1, keepdims=True)
    grad_time_part = jnp.concatenate(
        [
            grad_shift_one,
            grad_scale_one,
            grad_gate_one,
            grad_shift_two,
            grad_scale_two,
            grad_gate_two,
        ],
        axis=1,
    ).reshape(latents, 6 * width)
    time_width = 6 * width // n_seq
    time_rows = -(-time_width // width)
    text_rows = text_len * group_width // width
    text_blocks = jnp.moveaxis(
        grad_text_part.astype(bf16).reshape(latents, text_len, n_seq, group_width), 2, 1
    ).reshape(latents, n_seq, text_rows, width)
    time_blocks = jnp.pad(
        grad_time_part.astype(bf16).reshape(latents, n_seq, time_width),
        ((0, 0), (0, 0), (0, time_rows * width - time_width)),
    ).reshape(latents, n_seq, time_rows, width)
    packed = jnp.concatenate(
        [
            grad_mod_one_part.astype(bf16).reshape(latents, n_seq, tokens, width),
            text_blocks,
            time_blocks,
        ],
        axis=2,
    ).reshape(latents, n_seq * (tokens + text_rows + time_rows), width)
    summed = lax.psum_scatter(packed, "seq", scatter_dimension=1, tiled=True).astype(f32)
    grad_mod_one = summed[:, :tokens]
    text_grad = summed[:, tokens : tokens + text_rows].reshape(latents, text_len, group_width)
    time_grad = summed[:, tokens + text_rows :].reshape(latents, time_rows * width)[:, :time_width]
    normed_one, recip_one = layer_norm(latent_in)
    latent_grad = grad_self + norm_back(grad_mod_one * (1.0 + scale_one), normed_one, recip_one)

    def own_cols(rows):
        return lax.dynamic_slice_in_dim(rows, me * group_width, group_width, axis=2)

    grad_cproj = dot("nblc,ble->nce", cross_all, own_cols(grad_cross_b)).reshape(width, group_width)
    grad_cquery_w = dot("bld,ble->de", after_self_b, grad_cq)
    grad_textkv_w = dot("bsd,mbse->mde", text_embed, grad_text_kv)
    grad_proj = dot("nblc,ble->nce", self_all, own_cols(grad_branch)).reshape(width, group_width)

    def reduce_rows(mats):
        part = jnp.concatenate([item.astype(bf16) for item in mats], axis=1)
        return lax.psum_scatter(part, "fsdp", scatter_dimension=0, tiled=True)

    def split_cols(rows, count):
        return jnp.moveaxis(rows.reshape(rows.shape[0], count, group_width), 1, 0)

    cross_sum = reduce_rows([grad_textkv_w[0], grad_textkv_w[1], grad_cquery_w, grad_cproj])
    cross_sum, grad_qkv, grad_proj = lax.optimization_barrier((cross_sum, grad_qkv, grad_proj))
    grad_qkv_w = dot("bld,sble->sde", mod_rows_one, grad_qkv)
    self_sum = reduce_rows([grad_qkv_w[0], grad_qkv_w[1], grad_qkv_w[2], grad_proj])
    cross_sum, self_sum = split_cols(cross_sum, 4), split_cols(self_sum, 4)
    textkv_grad = cross_sum[0:2].astype(f32)
    attn_grad = jnp.concatenate([self_sum, cross_sum[2:4]], axis=0).astype(f32)
    table_grad = lax.psum(jnp.sum(time_grad, axis=0), "fsdp")
    attn_new, attn_first_new, attn_second_new = adamw(
        attn_weight, attn_first, attn_second, attn_grad
    )
    textkv_new, textkv_first_new, textkv_second_new = adamw(
        textkv_weight, textkv_first, textkv_second, textkv_grad
    )
    mlp_new, mlp_first_new, mlp_second_new = adamw(mlp_weight, mlp_first, mlp_second, mlp_grad)
    table_new, table_first_new, table_second_new = adamw(
        table_weight, table_first, table_second, table_grad
    )
    return (
        block_out,
        latent_grad,
        text_grad,
        time_grad,
        attn_grad,
        textkv_grad,
        mlp_grad,
        table_grad,
        attn_new,
        textkv_new,
        mlp_new,
        table_new,
        attn_first_new,
        textkv_first_new,
        mlp_first_new,
        table_first_new,
        attn_second_new,
        textkv_second_new,
        mlp_second_new,
        table_second_new,
    )


def solution(mesh):
    in_specs = (
        P("fsdp", "seq", None),
        P("fsdp", None),
        P("fsdp", None, None),
        P("fsdp", "seq", None),
        P(None, "fsdp", "seq"),
        P(None, "fsdp", "seq"),
        P(None, "fsdp", "seq"),
        P(None, "fsdp", "seq"),
        P(None, "fsdp", "seq"),
        P(None, "fsdp", "seq"),
        P(None, "fsdp", "seq"),
        P(None, "fsdp", "seq"),
        P(None, "fsdp", "seq"),
        P("seq"),
        P("seq"),
        P("seq"),
    )
    out_specs = (
        P("fsdp", "seq", None),
        P("fsdp", "seq", None),
        P("fsdp", None, "seq"),
        P("fsdp", "seq"),
        P(None, "fsdp", "seq"),
        P(None, "fsdp", "seq"),
        P(None, "fsdp", "seq"),
        P("seq"),
        P(None, "fsdp", "seq"),
        P(None, "fsdp", "seq"),
        P(None, "fsdp", "seq"),
        P("seq"),
        P(None, "fsdp", "seq"),
        P(None, "fsdp", "seq"),
        P(None, "fsdp", "seq"),
        P("seq"),
        P(None, "fsdp", "seq"),
        P(None, "fsdp", "seq"),
        P(None, "fsdp", "seq"),
        P("seq"),
    )
    return jax.shard_map(body, mesh=mesh, in_specs=in_specs, out_specs=out_specs, check_vma=False)
```

```python
import functools
import math

import jax
import jax.numpy as jnp
from jax import lax
from jax.experimental import pallas as pl
from jax.experimental.pallas import tpu as pltpu
from jax.sharding import PartitionSpec as P

HEAD_DIM = 72


norm_eps = 1e-06
gelu_coef = 0.7978845608028654
gelu_cube = 0.044715
beta_first = 0.9
beta_second = 0.999
adam_eps = 1e-08
learn_rate = 0.05
weight_decay = 0.01
fix_first = 1.0 - 0.9**10
fix_second = 1.0 - 0.999**10


def layer_norm(rows):
    centre = rows - jnp.mean(rows, axis=-1, keepdims=True)
    recip = lax.rsqrt(jnp.mean(centre * centre, axis=-1, keepdims=True) + norm_eps)
    return (centre * recip, recip)


def norm_back(grad_norm, normed, recip):
    return recip * (
        grad_norm
        - jnp.mean(grad_norm, axis=-1, keepdims=True)
        - normed * jnp.mean(grad_norm * normed, axis=-1, keepdims=True)
    )


def gelu_pair(hidden):
    inner = gelu_coef * (hidden + gelu_cube * hidden * hidden * hidden)
    tangent = jnp.tanh(inner)
    value_out = 0.5 * hidden * (1.0 + tangent)
    slope = 0.5 * (1.0 + tangent) + 0.5 * hidden * (1.0 - tangent * tangent) * gelu_coef * (
        1.0 + 3.0 * gelu_cube * hidden * hidden
    )
    return (value_out, slope)


def adamw(weight, moment, second, gradient):
    moment_new = beta_first * moment + (1.0 - beta_first) * gradient
    second_new = beta_second * second + (1.0 - beta_second) * gradient * gradient
    update = moment_new / fix_first / (jnp.sqrt(second_new / fix_second) + adam_eps)
    return (weight - learn_rate * (update + weight_decay * weight), moment_new, second_new)


def line_gather_kernel(n, count, *refs):
    sources, targets = refs[:count], refs[count : 2 * count]
    local_sem, send_right, recv_right, send_left, recv_left = refs[2 * count :]
    me = lax.axis_index("seq")
    barrier = pltpu.get_barrier_semaphore()

    @pl.when(me > 0)
    def _():
        pl.semaphore_signal(barrier, inc=1, device_id={"seq": me - 1})

    @pl.when(me < n - 1)
    def _():
        pl.semaphore_signal(barrier, inc=1, device_id={"seq": me + 1})

    own = [
        pltpu.make_async_copy(source, target.at[me], local_sem.at[item])
        for item, (source, target) in enumerate(zip(sources, targets))
    ]
    for copy in own:
        copy.start()

    pl.semaphore_wait(barrier, jnp.where(me > 0, 1, 0) + jnp.where(me < n - 1, 1, 0))

    def hop(item, step, right):
        block = me - step if right else me + step
        source = sources[item] if step == 0 else targets[item].at[block]
        sends, receives = (send_right, recv_right) if right else (send_left, recv_left)
        return pltpu.make_async_remote_copy(
            src_ref=source,
            dst_ref=targets[item].at[block],
            send_sem=sends.at[item, step],
            recv_sem=receives.at[item, step],
            device_id={"seq": me + 1 if right else me - 1},
        )

    def arrival(item, step, right):
        block = me - 1 - step if right else me + 1 + step
        sends, receives = (send_right, recv_right) if right else (send_left, recv_left)
        return pltpu.make_async_copy(
            sources[item], targets[item].at[block], receives.at[item, step]
        )

    def sends_right(step):
        return jnp.logical_and(me - step >= 0, me < n - 1)

    def sends_left(step):
        return jnp.logical_and(me + step < n, me > 0)

    for step in range(n - 1):
        for item in range(count):

            @pl.when(sends_right(step))
            def _():
                hop(item, step, True).start()

            @pl.when(sends_left(step))
            def _():
                hop(item, step, False).start()

        for item in range(count):

            @pl.when(me - 1 - step >= 0)
            def _():
                arrival(item, step, True).wait()

            @pl.when(me + 1 + step < n)
            def _():
                arrival(item, step, False).wait()

    for step in range(n - 1):
        for item in range(count):

            @pl.when(sends_right(step))
            def _():
                hop(item, step, True).wait_send()

            @pl.when(sends_left(step))
            def _():
                hop(item, step, False).wait_send()

    for copy in own:
        copy.wait()


def line_gather(ident, *arrays):
    n = lax.axis_size("seq")
    count = len(arrays)
    anywhere = pl.BlockSpec(memory_space=pl.ANY)
    return pl.pallas_call(
        functools.partial(line_gather_kernel, n, count),
        out_shape=[jax.ShapeDtypeStruct((n,) + a.shape, a.dtype) for a in arrays],
        in_specs=[anywhere] * count,
        out_specs=[anywhere] * count,
        scratch_shapes=[pltpu.SemaphoreType.DMA((count,))]
        + [pltpu.SemaphoreType.DMA((count, n - 1))] * 4,
        compiler_params=pltpu.CompilerParams(collective_id=ident, has_side_effects=True),
    )(*arrays)


def attend(query_rows, key_rows, value_rows, block):
    latents, length, group, width = query_rows.shape
    count = length // block
    pieces = jnp.moveaxis(query_rows.reshape(latents, count, block, group, width), 1, 0)

    def one_block(piece):
        scores = jnp.einsum(
            "bqgd,bkgd->bgqk", piece, key_rows, preferred_element_type=jnp.float32
        ) * width ** (-0.5)
        row_max = jnp.max(scores, axis=-1, keepdims=True)
        log_total = row_max + jnp.log(jnp.sum(jnp.exp(scores - row_max), axis=-1, keepdims=True))
        soft_b = jnp.exp(scores - log_total).astype(jnp.bfloat16)
        output = jnp.einsum(
            "bgqk,bkgd->bqgd", soft_b, value_rows, preferred_element_type=jnp.float32
        ).astype(jnp.bfloat16)
        return (output, log_total)

    outputs, totals = lax.map(one_block, pieces)
    return (jnp.moveaxis(outputs, 0, 1).reshape(query_rows.shape), totals)


def attend_back(query_rows, key_rows, value_rows, totals, grad_rows, block):
    latents, length, group, width = query_rows.shape
    count = length // block
    query_pieces = jnp.moveaxis(query_rows.reshape(latents, count, block, group, width), 1, 0)
    grad_pieces = jnp.moveaxis(grad_rows.reshape(latents, count, block, group, width), 1, 0)

    def one_block(carry, item):
        piece, grad_piece, log_total = item
        scores = jnp.einsum(
            "bqgd,bkgd->bgqk", piece, key_rows, preferred_element_type=jnp.float32
        ) * width ** (-0.5)
        soft = jnp.exp(scores - log_total)
        grad_soft = jnp.einsum(
            "bqgd,bkgd->bgqk", grad_piece, value_rows, preferred_element_type=jnp.float32
        )
        row_dot = jnp.sum(soft * grad_soft, axis=-1, keepdims=True)
        grad_score = (soft * (grad_soft - row_dot) * width ** (-0.5)).astype(jnp.bfloat16)
        grad_query = jnp.einsum(
            "bgqk,bkgd->bqgd", grad_score, key_rows, preferred_element_type=jnp.float32
        ).astype(jnp.bfloat16)
        grad_key = carry[0] + jnp.einsum(
            "bgqk,bqgd->bkgd", grad_score, piece, preferred_element_type=jnp.float32
        )
        grad_value = carry[1] + jnp.einsum(
            "bgqk,bqgd->bkgd",
            soft.astype(jnp.bfloat16),
            grad_piece,
            preferred_element_type=jnp.float32,
        )
        return ((grad_key, grad_value), grad_query)

    zeros = jnp.zeros(key_rows.shape, jnp.float32)
    (grad_key, grad_value), grad_query = lax.scan(
        one_block, (zeros, zeros), (query_pieces, grad_pieces, totals)
    )
    grad_query = jnp.moveaxis(grad_query, 0, 1).reshape(query_rows.shape)
    return (grad_query, grad_key.astype(jnp.bfloat16), grad_value.astype(jnp.bfloat16))


def body(
    latent_in,
    time_embed,
    text_embed,
    grad_out,
    attn_weight,
    attn_first,
    attn_second,
    textkv_weight,
    textkv_first,
    textkv_second,
    mlp_weight,
    mlp_first,
    mlp_second,
    table_weight,
    table_first,
    table_second,
):
    n_seq = lax.axis_size("seq")
    me = lax.axis_index("seq")
    latents, tokens, width = latent_in.shape
    text_len = text_embed.shape[1]
    length = tokens * n_seq
    group_width = width // n_seq
    group = group_width // HEAD_DIM
    block = math.gcd(length, 512)
    f32, bf16 = jnp.float32, jnp.bfloat16
    attn_b = attn_weight.astype(bf16)
    text_b = textkv_weight.astype(bf16)

    def dot(spec, left, right):
        return jnp.einsum(spec, left, right, preferred_element_type=f32)

    def join_tokens(blocks):
        return jnp.moveaxis(blocks, 0, 1).reshape(latents, length, blocks.shape[-1])

    def own_tokens(rows):
        return lax.dynamic_slice_in_dim(rows, me * tokens, tokens, axis=1)

    cols_full = lax.all_gather(
        jnp.concatenate([attn_b[0:3], text_b, attn_b[4:5]], axis=0), "fsdp", axis=1, tiled=True
    )
    out_pieces, latent_all, table_all = line_gather(
        0,
        attn_b[3:6],
        latent_in.astype(bf16),
        table_weight.astype(bf16)[None, :],
    )
    out_rows = jnp.moveaxis(out_pieces, 0, 2).reshape(3, attn_b.shape[1], width)
    out_rows, cols_full = lax.optimization_barrier((out_rows, cols_full))
    out_full = lax.all_gather(out_rows, "fsdp", axis=1, tiled=True)

    modulation = (time_embed + table_all.reshape(1, -1).astype(f32)).reshape(latents, 6, width)
    shift_one, scale_one, gate_one, shift_two, scale_two, gate_two = jnp.split(
        modulation, 6, axis=1
    )
    latent_rows = join_tokens(latent_all).astype(f32)
    normed_rows, _ = layer_norm(latent_rows)
    mod_rows_one = (normed_rows * (1.0 + scale_one) + shift_one).astype(bf16)
    qkv = dot("bld,sde->sble", mod_rows_one, cols_full[0:3]).astype(bf16)
    query_rows = qkv[0].reshape(latents, length, group, HEAD_DIM)
    key_rows = qkv[1].reshape(latents, length, group, HEAD_DIM)
    value_rows = qkv[2].reshape(latents, length, group, HEAD_DIM)
    self_out, self_total = attend(query_rows, key_rows, value_rows, block)
    self_all, grad_all = line_gather(
        1,
        self_out.reshape(latents, length, group_width),
        grad_out.astype(bf16),
    )
    mlp_b, out_full, self_all = lax.optimization_barrier(
        (mlp_weight.astype(bf16), out_full, self_all)
    )
    mlp_full = lax.all_gather(mlp_b, "fsdp", axis=1, tiled=True)
    proj_rows = out_full[0].reshape(n_seq, group_width, width)
    cproj_rows = out_full[2].reshape(n_seq, group_width, width)
    branch = dot("nblc,nce->ble", self_all, proj_rows)
    after_self = latent_rows + gate_one * branch
    after_self_b = after_self.astype(bf16)
    cross_query = (
        dot("bld,de->ble", after_self_b, cols_full[5])
        .astype(bf16)
        .reshape(latents, length, group, HEAD_DIM)
    )
    text_kv = dot("bsd,mde->mbse", text_embed, cols_full[3:5]).astype(bf16)
    text_keys = text_kv[0].reshape(latents, text_len, group, HEAD_DIM)
    text_values = text_kv[1].reshape(latents, text_len, group, HEAD_DIM)
    cross_out, cross_total = attend(cross_query, text_keys, text_values, block)
    (cross_all,) = line_gather(2, cross_out.reshape(latents, length, group_width))
    cross_branch = dot("nblc,nce->ble", cross_all, cproj_rows)
    after_cross = after_self + cross_branch
    own_branch = own_tokens(branch)
    own_after = latent_in + gate_one * own_branch + own_tokens(cross_branch)
    normed_two, recip_two = layer_norm(own_after)
    normed_all, _ = layer_norm(after_cross)
    mod_rows = (normed_all * (1.0 + scale_two) + shift_two).astype(bf16)
    hidden = dot("bld,df->blf", mod_rows, mlp_full[0])
    activated, slope = gelu_pair(hidden)
    activated_b = activated.astype(bf16)
    grad_mlp_rows = (gate_two * join_tokens(grad_all).astype(f32)).astype(bf16)
    grad_act = dot("bld,df->blf", grad_mlp_rows, mlp_full[1])
    grad_hidden = (grad_act * slope).astype(bf16)
    grad_mod_part = dot("blf,df->bld", grad_hidden, mlp_full[0])
    grad_mod_two = lax.psum_scatter(
        grad_mod_part.astype(bf16), "seq", scatter_dimension=1, tiled=True
    ).astype(f32)
    grad_down = dot("bld,blf->df", grad_mlp_rows, activated_b)
    grad_up = dot("bld,blf->df", mod_rows, grad_hidden)
    partial_out = dot("blf,df->bld", activated_b, mlp_full[1])
    grad_gate_two = jnp.sum(join_tokens(grad_all).astype(f32) * partial_out, axis=1, keepdims=True)
    partial_out = partial_out.astype(bf16)
    grad_mlp_part = jnp.stack([grad_up.astype(bf16), grad_down.astype(bf16)])
    grad_mod_two, partial_out, grad_mlp_part = lax.optimization_barrier(
        (grad_mod_two, partial_out, grad_mlp_part)
    )
    mlp_sum = lax.psum_scatter(grad_mlp_part, "fsdp", scatter_dimension=1, tiled=True)
    mlp_out = lax.psum_scatter(partial_out, "seq", scatter_dimension=1, tiled=True)
    grad_scale_two = jnp.sum(grad_mod_two * normed_two, axis=1, keepdims=True)
    grad_shift_two = jnp.sum(grad_mod_two, axis=1, keepdims=True)
    grad_cross = grad_out + norm_back(grad_mod_two * (1.0 + scale_two), normed_two, recip_two)
    (grad_cross_all,) = line_gather(3, grad_cross.astype(bf16))
    grad_cross_b = join_tokens(grad_cross_all)
    own_cproj = lax.dynamic_index_in_dim(cproj_rows, me, axis=0, keepdims=False)
    own_proj = lax.dynamic_index_in_dim(proj_rows, me, axis=0, keepdims=False)
    grad_cross_heads = (
        dot("ble,ce->blc", grad_cross_b, own_cproj)
        .astype(bf16)
        .reshape(latents, length, group, HEAD_DIM)
    )
    grad_cq, grad_tk, grad_tv = attend_back(
        cross_query, text_keys, text_values, cross_total, grad_cross_heads, block
    )
    grad_cq = grad_cq.reshape(latents, length, group_width)
    grad_cq_blocks = lax.all_to_all(
        jnp.moveaxis(grad_cq.reshape(latents, n_seq, tokens, group_width), 1, 0),
        "seq",
        split_axis=0,
        concat_axis=0,
        tiled=True,
    )
    grad_cq_rows = jnp.moveaxis(grad_cq_blocks, 0, 2).reshape(latents, tokens, width)
    grad_self = grad_cross + dot("bte,de->btd", grad_cq_rows, out_full[1])
    grad_gate_one = jnp.sum(grad_self * own_branch, axis=1, keepdims=True)
    own_grad, mlp_sum = lax.optimization_barrier(((gate_one * grad_self).astype(bf16), mlp_sum))
    (grad_branch_all,) = line_gather(4, own_grad)
    grad_branch = join_tokens(grad_branch_all)
    grad_self_heads = (
        dot("ble,ce->blc", grad_branch, own_proj)
        .astype(bf16)
        .reshape(latents, length, group, HEAD_DIM)
    )
    grad_q, grad_k, grad_v = attend_back(
        query_rows, key_rows, value_rows, self_total, grad_self_heads, block
    )
    grad_qkv = jnp.stack([item.reshape(latents, length, group_width) for item in (grad_q, grad_k, grad_v)])
    grad_mod_one_part = dot("sble,sde->bld", grad_qkv, cols_full[0:3])
    grad_tk = grad_tk.reshape(latents, text_len, group_width)
    grad_tv = grad_tv.reshape(latents, text_len, group_width)
    grad_text_kv = jnp.stack([grad_tk, grad_tv])
    grad_text_part = dot("mbse,mde->bsd", grad_text_kv, cols_full[3:5])
    grad_scale_one = jnp.sum(grad_mod_one_part * normed_rows, axis=1, keepdims=True)
    grad_shift_one = jnp.sum(grad_mod_one_part, axis=1, keepdims=True)
    grad_time_part = jnp.concatenate(
        [
            grad_shift_one,
            grad_scale_one,
            grad_gate_one,
            grad_shift_two,
            grad_scale_two,
            grad_gate_two,
        ],
        axis=1,
    ).reshape(latents, 6 * width)
    time_width = 6 * width // n_seq
    time_rows = -(-time_width // width)
    text_rows = text_len * group_width // width
    text_blocks = jnp.moveaxis(
        grad_text_part.astype(bf16).reshape(latents, text_len, n_seq, group_width), 2, 1
    ).reshape(latents, n_seq, text_rows, width)
    time_blocks = jnp.pad(
        grad_time_part.astype(bf16).reshape(latents, n_seq, time_width),
        ((0, 0), (0, 0), (0, time_rows * width - time_width)),
    ).reshape(latents, n_seq, time_rows, width)
    packed = jnp.concatenate(
        [
            grad_mod_one_part.astype(bf16).reshape(latents, n_seq, tokens, width),
            text_blocks,
            time_blocks,
        ],
        axis=2,
    )

    def own_cols(rows):
        return lax.dynamic_slice_in_dim(rows, me * group_width, group_width, axis=2)

    grad_cproj = dot("nblc,ble->nce", cross_all, own_cols(grad_cross_b)).reshape(width, group_width)
    grad_cquery_w = dot("bld,ble->de", after_self_b, grad_cq)
    grad_textkv_w = dot("bsd,mbse->mde", text_embed, grad_text_kv)
    grad_proj = dot("nblc,ble->nce", self_all, own_cols(grad_branch)).reshape(width, group_width)

    def join_mats(mats):
        return jnp.concatenate([item.astype(bf16) for item in mats], axis=1)

    def split_cols(rows, count):
        return jnp.moveaxis(rows.reshape(rows.shape[0], count, group_width), 1, 0)

    cross_part, mlp_sum = lax.optimization_barrier(
        (join_mats([grad_textkv_w[0], grad_textkv_w[1], grad_cquery_w, grad_cproj]), mlp_sum)
    )
    cross_sum = lax.psum_scatter(cross_part, "fsdp", scatter_dimension=0, tiled=True)
    cross_sum, grad_qkv, grad_proj = lax.optimization_barrier((cross_sum, grad_qkv, grad_proj))
    grad_qkv_w = dot("bld,sble->sde", mod_rows_one, grad_qkv)
    self_part = join_mats([grad_qkv_w[0], grad_qkv_w[1], grad_qkv_w[2], grad_proj])
    self_part, packed, mlp_out = lax.optimization_barrier((self_part, packed, mlp_out))
    block_out = own_after + gate_two * mlp_out.astype(f32)
    self_sum = lax.psum_scatter(self_part, "fsdp", scatter_dimension=0, tiled=True)
    summed = jnp.sum(
        lax.all_to_all(packed, "seq", split_axis=1, concat_axis=1, tiled=True).astype(f32), axis=1
    )
    grad_mod_one = summed[:, :tokens]
    text_grad = summed[:, tokens : tokens + text_rows].reshape(latents, text_len, group_width)
    time_grad = summed[:, tokens + text_rows :].reshape(latents, time_rows * width)[:, :time_width]
    normed_one, recip_one = layer_norm(latent_in)
    latent_grad = grad_self + norm_back(grad_mod_one * (1.0 + scale_one), normed_one, recip_one)
    cross_sum, self_sum = split_cols(cross_sum, 4), split_cols(self_sum, 4)
    mlp_grad = mlp_sum.astype(f32)
    textkv_grad = cross_sum[0:2].astype(f32)
    attn_grad = jnp.concatenate([self_sum, cross_sum[2:4]], axis=0).astype(f32)
    table_grad = lax.psum(jnp.sum(time_grad, axis=0), "fsdp")
    attn_new, attn_first_new, attn_second_new = adamw(
        attn_weight, attn_first, attn_second, attn_grad
    )
    textkv_new, textkv_first_new, textkv_second_new = adamw(
        textkv_weight, textkv_first, textkv_second, textkv_grad
    )
    mlp_new, mlp_first_new, mlp_second_new = adamw(mlp_weight, mlp_first, mlp_second, mlp_grad)
    table_new, table_first_new, table_second_new = adamw(
        table_weight, table_first, table_second, table_grad
    )
    return (
        block_out,
        latent_grad,
        text_grad,
        time_grad,
        attn_grad,
        textkv_grad,
        mlp_grad,
        table_grad,
        attn_new,
        textkv_new,
        mlp_new,
        table_new,
        attn_first_new,
        textkv_first_new,
        mlp_first_new,
        table_first_new,
        attn_second_new,
        textkv_second_new,
        mlp_second_new,
        table_second_new,
    )


def solution(mesh):
    in_specs = (
        P("fsdp", "seq", None),
        P("fsdp", None),
        P("fsdp", None, None),
        P("fsdp", "seq", None),
        P(None, "fsdp", "seq"),
        P(None, "fsdp", "seq"),
        P(None, "fsdp", "seq"),
        P(None, "fsdp", "seq"),
        P(None, "fsdp", "seq"),
        P(None, "fsdp", "seq"),
        P(None, "fsdp", "seq"),
        P(None, "fsdp", "seq"),
        P(None, "fsdp", "seq"),
        P("seq"),
        P("seq"),
        P("seq"),
    )
    out_specs = (
        P("fsdp", "seq", None),
        P("fsdp", "seq", None),
        P("fsdp", None, "seq"),
        P("fsdp", "seq"),
        P(None, "fsdp", "seq"),
        P(None, "fsdp", "seq"),
        P(None, "fsdp", "seq"),
        P("seq"),
        P(None, "fsdp", "seq"),
        P(None, "fsdp", "seq"),
        P(None, "fsdp", "seq"),
        P("seq"),
        P(None, "fsdp", "seq"),
        P(None, "fsdp", "seq"),
        P(None, "fsdp", "seq"),
        P("seq"),
        P(None, "fsdp", "seq"),
        P(None, "fsdp", "seq"),
        P(None, "fsdp", "seq"),
        P("seq"),
    )
    return jax.shard_map(body, mesh=mesh, in_specs=in_specs, out_specs=out_specs, check_vma=False)
```
